512 devices in a mesh: aperture: 32 (over y, x, core), beam: 16 (over z).
Axes of the slice: x: 4, y: 4, z: 16, core: 2. Of those that a mesh axis runs over, the one named last changes fastest.
Arguments:
- subimages: bfloat16 [32, 2, 4096, 512], P('aperture', None, 'beam'), may hold values from -6 to 6
- range_kernel: bfloat16 [32, 2, 512, 512], P('aperture'), may hold values from -0.1875 to 0.1875
- weights0: bfloat16 [32, 64, 2, 128, 320], P('aperture', 'beam'), may hold values from -0.25 to 0.25
- starts0: int32 [32, 64], P(None, 'beam'), may hold values from -6 to 124, as said below
- weights1: bfloat16 [32, 128, 2, 128, 320], P('aperture', 'beam'), may hold values from -0.25 to 0.25
- starts1: int32 [32, 128], P(None, 'beam'), may hold values from -6 to 252, as said below
- owners: int32 [32, 256, 1], P('aperture', 'beam'), may hold values from 0 to 15; in each aligned block of 16 rows (0 to 15, 16 to 31, ..., all dimensions but the last counted through in order) at most 2 rows name the same one
Outputs:
- merged: bfloat16 [32, 512, 2, 64, 128], P('aperture', 'beam')
The draws below stay inside these ranges and needn't reach their ends.
Inputs may be any that keep to these rules, and one draw needn't show every extreme that they name: starts0[s, p] = 2p - (10 - 2) // 2 + e with -2 <= e <= 2; both ends of e occur. starts1[s, p] = 2p - (10 - 2) // 2 + e with -2 <= e <= 2; both ends of e occur. `owners`: among the 16 sectors homed on one beam device (aligned blocks of 16 rows of one subaperture row), at most 2 name the same owner, a bound that some block reaches.
All inputs are finite; a program needn't handle non-finite values.
Results may differ from the reference program's by a relative error of at most 0.0072.
Values may be sent and summed in bfloat16 or wider, within the bound.
A program may use at most 64 MiB of HBM per device.

```python
import math
import jax
import jax.numpy as jnp
import numpy as np
from jax import lax

BLK = 32
NW = 10
REACH = 2
BDEV_BLK = 8
RNG = 512
S = 32
PS = 128
OS = 64
WIN = 320
CB0 = 4096
NSEC0 = 64
NSEC1 = 128
ODEV = 16
ONS = 256
CAP = 2
SLOTS = 512
HALF = 256
QUART = 128
N_BEAM = 16


def start_table(key, row_count, sectors, per_device):
    subkeys = jax.random.split(key, 7)
    offset = jax.random.randint(subkeys[0], (row_count, sectors), -REACH, REACH + 1)
    low_row = jax.random.randint(subkeys[1], (), 0, row_count)
    low_device = jax.random.randint(subkeys[2], (), 0, sectors // per_device)
    high_row = jax.random.randint(subkeys[3], (), 0, row_count)
    high_device = jax.random.randint(subkeys[4], (), 0, sectors // per_device)
    first_row = jax.random.randint(subkeys[5], (), 0, row_count)
    last_row = jax.random.randint(subkeys[6], (), 0, row_count)
    row_index = jnp.arange(row_count, dtype=jnp.int32)[:, None]
    sector_index = jnp.arange(sectors, dtype=jnp.int32)[None, :]
    offset = jnp.where((row_index == low_row) & (sector_index == low_device * per_device), -REACH, offset)
    offset = jnp.where((row_index == high_row) & (sector_index == high_device * per_device + per_device - 1), REACH, offset)
    offset = jnp.where((row_index == first_row) & (sector_index == 0), -REACH, offset)
    offset = jnp.where((row_index == last_row) & (sector_index == sectors - 1), REACH, offset)
    return (2 * sector_index - (NW - 2) // 2 + offset).astype(jnp.int32)


def draw_starts0(key, part):
    return start_table(jax.random.fold_in(key, 11), S, NSEC0, BDEV_BLK // 2)


def draw_starts1(key, part):
    return start_table(jax.random.fold_in(key, 23), S, NSEC1, BDEV_BLK)


def level_of(stream_key, shape, cuts, least, top_value):
    def one(position, parts):
        heights = jax.random.uniform(jax.random.fold_in(jax.random.fold_in(stream_key, 6), position), (parts,), jnp.float32, least / len(cuts), top_value / len(cuts))
        return jnp.repeat(jnp.exp(heights), shape[position] // parts).reshape((-1,) + (1,) * (len(shape) - position - 1))

    factor_of = one(*cuts[0])
    for cut in cuts[1:]:
        factor_of = factor_of * one(*cut)
    return factor_of


def deal_out(stream_key, own, number, rows, count, top, bound, slope):
    ranking = jax.random.permutation(stream_key, count)
    packed, common = portions_of(count, rows * top, bound, slope, True), portions_of(count, rows * top, bound, slope, False)
    places = jnp.arange(count)

    def named(sizes, offset_by):
        used = int((sizes > 0).sum())
        fixed = max(1, used // 4)
        shifted = fixed + (places - fixed + offset_by * (used - fixed)) % max(1, count - fixed)
        return jnp.zeros((count,), jnp.int32).at[ranking[jnp.where(places < fixed, places, shifted)]].set(jnp.asarray(sizes, jnp.int32))

    sizes = jnp.where(number % 4 == 0, named(packed, number // 4), named(common, number - number // 4 - 1))
    mixed = jax.random.permutation(jax.random.fold_in(own, 3), count)
    source_of, taker = mixed[0:count // 2 * 2:2], mixed[1:count // 2 * 2:2]
    slack = jnp.minimum(sizes[source_of] - 1, bound - sizes[taker]) // 2
    slack = jnp.where((source_of == ranking[0]) | (taker == ranking[0]) | (sizes[taker] == 0), 0, jnp.maximum(slack, 0))
    shifted = jax.random.randint(jax.random.fold_in(own, 4), (count // 2,), 0, 1 << 20) % (slack + 1)
    sizes = sizes.at[source_of].add(-shifted).at[taker].add(shifted)
    items = jnp.searchsorted(jnp.cumsum(sizes), jnp.arange(rows * top), side="right").astype(jnp.int32)
    grid = items.reshape(top, rows).T
    grid = grid[jax.random.permutation(jax.random.fold_in(own, 1), rows)]
    offset_by = jax.random.randint(jax.random.fold_in(own, 2), (rows, 1), 0, top)
    return jnp.take_along_axis(grid, (jnp.arange(top)[None, :] + offset_by) % top, axis=1)


def portions_of(amount, total, limit, slope, full):
    loads = [(1 << 20) // math.isqrt(rank ** slope) + 1 for rank in range(1, amount + 1)]
    largest = limit if full else min(limit, max(-(-total // amount), total * loads[0] // sum(loads)))
    least = 1 if total - largest >= amount - 1 else 0
    holding, surplus = [largest] + [least] * (amount - 1), total - largest - least * (amount - 1)
    while surplus > 0:
        candidates = [i for i in range(1, amount) if holding[i] < largest] or [i for i in range(1, amount) if holding[i] < limit]
        mass, left = sum([loads[i] for i in candidates]), surplus
        for i in candidates:
            extra = min(limit - holding[i], max(1, left * loads[i] // mass), surplus)
            holding[i] = holding[i] + extra
            surplus = surplus - extra
    return np.array(holding)


def gaussian(stream_key, dims, width, reach, shards=(), held_as=jnp.bfloat16):
    level = level_of(stream_key, dims, shards, -0.22, 0.18) if shards else 1.0
    result = jax.random.normal(stream_key, dims, jnp.float32) * width * level
    return jnp.minimum(jnp.maximum(result, -reach), reach).astype(held_as)


def setup_inputs(seed: int = 0) -> dict:
    splits = jax.random.split(jax.random.key(seed), 8)
    subimages = gaussian(splits[0], (S, 2, CB0, RNG), 1.0, 6.0, ((0, 32), (2, 16)))
    range_kernel = gaussian(splits[1], (S, 2, RNG, RNG), (2 * RNG) ** -0.5, 0.1875, ((0, 32),))
    weights0 = gaussian(splits[2], (S, NSEC0, 2, PS, WIN), (2 * WIN) ** -0.5, 0.25, ((0, 32), (1, 16)))
    starts0 = draw_starts0(jax.random.fold_in(splits[7], 71), 0)
    weights1 = gaussian(splits[4], (S, NSEC1, 2, PS, WIN), (2 * WIN) ** -0.5, 0.25, ((0, 32), (1, 16)))
    starts1 = draw_starts1(jax.random.fold_in(splits[7], 71), 0)
    owners_keys = jax.random.split(jax.random.fold_in(splits[6], 1), S * ONS // ODEV)
    owners_turns = jax.random.permutation(jax.random.fold_in(splits[6], 3), S * ONS // ODEV)
    owners = jax.vmap(lambda own, number: deal_out(jax.random.fold_in(splits[6], 2), own, number, ODEV, N_BEAM, 1, CAP, 2))(owners_keys, owners_turns).reshape((S, ONS, 1))
    return {"subimages": subimages, "range_kernel": range_kernel, "weights0": weights0, "starts0": starts0, "weights1": weights1, "starts1": starts1, "owners": owners}


def complex_dot(left_real, left_imag, right_real, right_imag):
    real_part = jnp.dot(left_real, right_real, preferred_element_type=jnp.float32) - jnp.dot(left_imag, right_imag, preferred_element_type=jnp.float32)
    imag_part = jnp.dot(left_real, right_imag, preferred_element_type=jnp.float32) + jnp.dot(left_imag, right_real, preferred_element_type=jnp.float32)
    return jnp.stack([real_part, imag_part])


def resample(operands):
    subimage, kernel = operands
    return complex_dot(subimage[0], subimage[1], kernel[0], kernel[1]).astype(jnp.bfloat16)


def interp(operands):
    child, weights, starts = operands
    margin = ((NW - 2) // 2 + REACH) * BLK
    padded = jnp.pad(child, ((0, 0), (margin, margin), (0, 0)))

    def one_sector(sector_operands):
        matrix, first_block = sector_operands
        window = lax.dynamic_slice_in_dim(padded, (first_block * BLK + margin).astype(jnp.int32), NW * BLK, 1)
        return complex_dot(matrix[0], matrix[1], window[0], window[1])

    sectors = lax.map(one_sector, (weights, starts))
    sector_count = sectors.shape[0]
    joined = jnp.transpose(sectors, (1, 0, 2, 3)).reshape(2, sector_count * sectors.shape[2], child.shape[2])
    return joined.astype(jnp.bfloat16)


def reference(subimages, range_kernel, weights0, starts0, weights1, starts1, owners):
    resampled = lax.map(resample, (subimages, range_kernel))
    beams_first = lax.map(interp, (resampled, weights0, starts0))
    level_one = (beams_first[0::2].astype(jnp.float32) + beams_first[1::2].astype(jnp.float32)).astype(jnp.bfloat16)
    width_one = level_one.shape[2]
    halves = level_one.reshape(S // 2, 2, width_one, 2, HALF).transpose(0, 3, 1, 2, 4).reshape(S, 2, width_one, HALF)
    beams_second = lax.map(interp, (halves, weights1, starts1))
    width_two = beams_second.shape[2]
    grouped = beams_second.astype(jnp.float32).reshape(S // 4, 2, 2, 2, width_two, HALF)
    summed = (grouped[:, 0] + grouped[:, 1]).astype(jnp.bfloat16)
    quarters = summed.reshape(S // 4, 2, 2, width_two, 2, QUART).transpose(0, 4, 1, 2, 3, 5).reshape(S, 2, width_two, QUART)
    by_sector = jnp.transpose(quarters.reshape(S, 2, ONS, OS, QUART), (0, 2, 1, 3, 4))
    target = owners[:, :, 0]
    one_hot = (target[:, :, None] == jnp.arange(N_BEAM, dtype=jnp.int32)[None, None, :]).astype(jnp.int32)
    grouped_hot = one_hot.reshape(S, N_BEAM, ODEV, N_BEAM)
    earlier = jnp.cumsum(grouped_hot, axis=2) - grouped_hot
    slot_rank = jnp.sum(earlier * grouped_hot, axis=3).reshape(S, ONS)
    home_device = jnp.arange(ONS, dtype=jnp.int32) // ODEV
    slot_index = (target * (N_BEAM * CAP) + home_device[None, :] * CAP + slot_rank).astype(jnp.int32)
    row_index = jnp.arange(S, dtype=jnp.int32)[:, None] * jnp.ones((1, ONS), jnp.int32)
    merged = jnp.zeros((S, SLOTS, 2, OS, QUART), jnp.bfloat16).at[row_index, slot_index].set(by_sector)
    return merged
```

```python
import jax
import jax.numpy as jnp
from jax import lax
from jax.experimental import pallas as pl
from jax.experimental.pallas import tpu as pltpu
from jax.sharding import PartitionSpec as P

BLK = 32
WIN = 320
PS = 128
OS = 64
NW = 10
RIM_BLK = 6
Q = 128
MESH = pl.DeviceIdType.MESH
BF16 = jnp.bfloat16
F32 = jnp.float32


def complex_product(left, right, rows):
    p = jnp.dot(left, right, preferred_element_type=F32)
    return p[:rows, :Q] - p[rows:, Q:], p[:rows, Q:] + p[rows:, :Q]


def kernel(
    sub, kern, w0h, w1h, st0, st1, own, out,
    x, kc, w0t, w1t, w0, w1, r0a, r0b, r0c, r0d, s0, q0, l1a, l1b, sx, rx, yo, qq, og,
    in_sem, k_sem, r_ssem, r_rsem, q_ssem, q_rsem, l_ssem, l_rsem, x_ssem, x_rsem, a_ssem, a_rsem, o_sem,
):
    ap = lax.axis_index("aperture")
    z = lax.axis_index("beam")
    n_beam = lax.axis_size("beam")
    h = lax.rem(ap, 2)
    t = lax.rem(ap // 2, 2)
    up = (ap, lax.rem(z + 1, n_beam))
    down = (ap, lax.rem(z + n_beam - 1, n_beam))
    core = (ap + 1 - 2 * h, z)
    across = (ap + 2 - 4 * t, z)
    first = z == 0
    last = z == n_beam - 1
    beams = x.shape[1]
    blocks0 = beams // BLK
    parts = [(1 - h) * 2 + 1 - t, h * 2 + 1 - t, (1 - h) * 2 + t, h * 2 + t]

    r0 = (r0a, r0b, r0c, r0d)
    l1 = (l1a, l1b)

    loads = [pltpu.make_async_copy(sub.at[0], x, in_sem.at[0])]
    loads[0].start()
    kloads = []
    for i in range(4):
        cols = pl.ds(pl.multiple_of(parts[i] * Q, Q), Q)
        for c in range(2):
            cp = pltpu.make_async_copy(kern.at[0, c, :, cols], kc.at[i, :, pl.ds(c * Q, Q)], k_sem.at[2 * i + c])
            cp.start()
            kloads.append(cp)
    for k, (src, dst) in enumerate(((w0h, w0t), (w1h, w1t))):
        cp = pltpu.make_async_copy(src.at[0], dst, in_sem.at[1 + k])
        cp.start()
        loads.append(cp)

    barrier = pltpu.get_barrier_semaphore()
    peers = [(ap, lax.rem(z + k, n_beam)) for k in range(1, n_beam)] + [core, across]
    for peer in peers:
        pl.semaphore_signal(barrier, inc=1, device_id=peer, device_id_type=MESH)

    def send(src, dst, ssem, rsem, peer):
        cp = pltpu.make_async_remote_copy(src, dst, ssem, rsem, device_id=peer, device_id_type=MESH)
        cp.start()
        return cp

    def rims(buf, i, blocks, ssem, rsem):
        low = send(buf[i].at[pl.ds(RIM_BLK, RIM_BLK)], buf[i].at[pl.ds(RIM_BLK + blocks, RIM_BLK)], ssem.at[i, 0], rsem.at[i, 0], down)
        high = send(buf[i].at[pl.ds(blocks, RIM_BLK)], buf[i].at[pl.ds(0, RIM_BLK)], ssem.at[i, 1], rsem.at[i, 1], up)
        return [low, high]

    def clear_ends(buf, i, blocks):
        @pl.when(first)
        def _():
            buf[i][pl.ds(0, RIM_BLK)] = jnp.zeros((RIM_BLK, BLK, 2 * Q), BF16)

        @pl.when(last)
        def _():
            buf[i][pl.ds(RIM_BLK + blocks, RIM_BLK)] = jnp.zeros((RIM_BLK, BLK, 2 * Q), BF16)

    r_cps = []
    loads[0].wait()
    for i in range(4):
        kloads[2 * i].wait()
        kloads[2 * i + 1].wait()
        re, im = complex_product(x[...].reshape(2 * beams, x.shape[2]), kc[i], beams)
        r0[i][pl.ds(RIM_BLK, blocks0), :, pl.ds(0, Q)] = re.astype(BF16).reshape(blocks0, BLK, Q)
        r0[i][pl.ds(RIM_BLK, blocks0), :, pl.ds(Q, Q)] = im.astype(BF16).reshape(blocks0, BLK, Q)
        if i == 0:
            pl.semaphore_wait(barrier, len(peers))
        r_cps.append(rims(r0, i, blocks0, r_ssem, r_rsem))

    places = []
    none = jnp.int32(own.shape[0])
    for k in range(n_beam):
        d = lax.rem(z + k, n_beam)
        one = two = none
        for o in reversed(range(own.shape[0])):
            hit = own[o] == d
            two = jnp.where(hit, one, two)
            one = jnp.where(hit, jnp.int32(o), one)
        places.append((one, two))
    qq[own.shape[0]] = jnp.zeros((OS, 2 * Q), BF16)

    def window(starts, j, blocks):
        at = starts[j, ap] - (blocks * z - RIM_BLK)
        return jnp.minimum(jnp.maximum(at, 2 * j), 2 * j + 4)

    def turn(src, dst, lo, hi):
        for j in range(lo, hi):
            for c in range(2):
                dst[j, c] = src[j, c].T

    n0 = w0.shape[0]
    n1 = w1.shape[0]
    loads[1].wait()
    turn(w0t, w0, 0, n0)
    loads[2].wait()
    blocks1 = n0 * PS // BLK
    q_cps = []
    l_cps = []
    for i in range(4):
        r_cps[i][0].wait_recv()
        r_cps[i][1].wait_recv()
        clear_ends(r0, i, blocks0)
        u = i // 2
        if i % 2:
            q_cps[u].wait_recv()
        for j in range(n0):
            at = window(st0, j, blocks0)
            re, im = complex_product(w0[j].reshape(2 * PS, WIN), r0[i][pl.ds(at, NW)].reshape(WIN, 2 * Q), PS)
            rows = pl.ds(j * PS, PS)
            if i % 2 == 0:
                s0[u, rows, pl.ds(0, Q)] = re.astype(BF16)
                s0[u, rows, pl.ds(Q, Q)] = im.astype(BF16)
            else:
                to = pl.ds(RIM_BLK + j * PS // BLK, PS // BLK)
                for part, lanes in ((re, pl.ds(0, Q)), (im, pl.ds(Q, Q))):
                    both = part.astype(BF16).astype(F32) + q0[u, rows, lanes].astype(F32)
                    l1[u][to, :, lanes] = both.astype(BF16).reshape(PS // BLK, BLK, Q)
        if i % 2 == 0:
            q_cps.append(send(s0.at[u], q0.at[u], q_ssem.at[u], q_rsem.at[u], core))
        else:
            l_cps.append(rims(l1, u, blocks1, l_ssem, l_rsem))
        if i < 2:
            turn(w1t, w1, i * n1 // 2, (i + 1) * n1 // 2)

    x_cps = []
    for u in range(2):
        l_cps[u][0].wait_recv()
        l_cps[u][1].wait_recv()
        clear_ends(l1, u, blocks1)
        for j in range(n1):
            at = window(st1, j, blocks1)
            re, im = complex_product(w1[j].reshape(2 * PS, WIN), l1[u][pl.ds(at, NW)].reshape(WIN, 2 * Q), PS)
            rows = pl.ds(j * PS, PS)
            dst = yo if u else sx
            dst[rows, pl.ds(0, Q)] = re.astype(BF16)
            dst[rows, pl.ds(Q, Q)] = im.astype(BF16)
            if u == 0:
                x_cps.append(send(sx.at[rows], rx.at[rows], x_ssem.at[j], x_rsem.at[j], across))
    for j in range(n1):
        rows = pl.ds(j * PS, PS)
        x_cps[j].wait_recv()
        both = yo[rows, :].astype(F32) + rx[rows, :].astype(F32)
        qq[pl.ds(j * PS // OS, PS // OS)] = both.astype(BF16).reshape(PS // OS, OS, 2 * Q)

    mine = pl.ds(2 * z, 2)
    a_cps = []
    order = [n_beam // 2]
    for k in range(n_beam // 2 - 1, 0, -1):
        order += [k, n_beam - k]
    for n, k in enumerate(order + [0]):
        d = lax.rem(z + k, n_beam)
        for c in range(2):
            sector = qq[places[k][c]]
            og[2 * d + c, 0] = sector[:, :Q]
            og[2 * d + c, 1] = sector[:, Q:]
        if k:
            a_cps.append(send(og.at[pl.ds(2 * d, 2)], out.at[mine], a_ssem.at[n], a_rsem.at[n], (ap, d)))
    local = pltpu.make_async_copy(og.at[mine], out.at[mine], o_sem)
    local.start()
    local.wait()
    for cp in a_cps:
        cp.wait()
    for cp in [c for pair in r_cps + l_cps for c in pair] + q_cps + x_cps:
        cp.wait_send()


def local(subimages, range_kernel, weights0, starts0, weights1, starts1, owners):
    beams, rng = subimages.shape[2], subimages.shape[3]
    n0, n1 = weights0.shape[1], weights1.shape[1]
    n_own = owners.shape[1]
    n_beam = lax.axis_size("beam")
    slots = 2 * n_beam
    hbm = pl.BlockSpec(memory_space=pl.ANY)
    smem = pl.BlockSpec(memory_space=pltpu.SMEM)
    dma = pltpu.SemaphoreType.DMA
    merged = pl.pallas_call(
        kernel,
        out_shape=jax.ShapeDtypeStruct((slots, 2, OS, Q), BF16),
        in_specs=[hbm, hbm, hbm, hbm, smem, smem, smem],
        out_specs=pl.BlockSpec(memory_space=pltpu.VMEM),
        scratch_shapes=[
            pltpu.VMEM((2, beams, rng), BF16),
            pltpu.VMEM((4, rng, 2 * Q), BF16),
            pltpu.VMEM((n0, 2, WIN, PS), BF16),
            pltpu.VMEM((n1, 2, WIN, PS), BF16),
            pltpu.VMEM((n0, 2, PS, WIN), BF16),
            pltpu.VMEM((n1, 2, PS, WIN), BF16),
            pltpu.VMEM((beams // BLK + 2 * RIM_BLK, BLK, 2 * Q), BF16),
            pltpu.VMEM((beams // BLK + 2 * RIM_BLK, BLK, 2 * Q), BF16),
            pltpu.VMEM((beams // BLK + 2 * RIM_BLK, BLK, 2 * Q), BF16),
            pltpu.VMEM((beams // BLK + 2 * RIM_BLK, BLK, 2 * Q), BF16),
            pltpu.VMEM((2, n0 * PS, 2 * Q), BF16),
            pltpu.VMEM((2, n0 * PS, 2 * Q), BF16),
            pltpu.VMEM((n0 * PS // BLK + 2 * RIM_BLK, BLK, 2 * Q), BF16),
            pltpu.VMEM((n0 * PS // BLK + 2 * RIM_BLK, BLK, 2 * Q), BF16),
            pltpu.VMEM((n1 * PS, 2 * Q), BF16),
            pltpu.VMEM((n1 * PS, 2 * Q), BF16),
            pltpu.VMEM((n1 * PS, 2 * Q), BF16),
            pltpu.VMEM((n1 * PS // OS + 1, OS, 2 * Q), BF16),
            pltpu.VMEM((slots, 2, OS, Q), BF16),
            dma((3,)),
            dma((8,)),
            dma((4, 2)),
            dma((4, 2)),
            dma((2,)),
            dma((2,)),
            dma((2, 2)),
            dma((2, 2)),
            dma((n1,)),
            dma((n1,)),
            dma((n_beam - 1,)),
            dma((n_beam - 1,)),
            dma,
        ],
        compiler_params=pltpu.CompilerParams(collective_id=0, has_side_effects=True),
    )(
        subimages,
        range_kernel,
        jnp.swapaxes(weights0, 3, 4),
        jnp.swapaxes(weights1, 3, 4),
        starts0.T,
        starts1.T,
        owners.reshape(n_own),
    )
    return merged[None]


def solution(mesh):
    return jax.shard_map(
        local,
        mesh=mesh,
        in_specs=(
            P("aperture", None, "beam", None),
            P("aperture", None, None, None),
            P("aperture", "beam", None, None, None),
            P(None, "beam"),
            P("aperture", "beam", None, None, None),
            P(None, "beam"),
            P("aperture", "beam", None),
        ),
        out_specs=P("aperture", "beam", None, None, None),
        check_vma=False,
    )
```

```python
import jax
import jax.numpy as jnp
from jax import lax
from jax.experimental import pallas as pl
from jax.experimental.pallas import tpu as pltpu
from jax.sharding import PartitionSpec as P

BLK = 32
WIN = 320
PS = 128
OS = 64
NW = 10
RIM_BLK = 6
Q = 128
MESH = pl.DeviceIdType.MESH
BF16 = jnp.bfloat16
F32 = jnp.float32


def complex_product(left, right, rows):
    p = jnp.dot(left, right, preferred_element_type=F32)
    return p[:rows, :Q] - p[rows:, Q:], p[:rows, Q:] + p[rows:, :Q]


def kernel(
    sub, kern, w0h, w1h, st0, st1, own, out,
    x, kc, w0t, w1t, w0, w1, r0a, r0b, r0c, r0d, s0, q0, l1a, l1b, sx, rx, px, yo, og, other,
    in_sem, k_sem, r_ssem, r_rsem, q_ssem, q_rsem, l_ssem, l_rsem, x_ssem, x_rsem, a_ssem, a_rsem, o_sem, o_ssem, o_rsem,
):
    ap = lax.axis_index("aperture")
    z = lax.axis_index("beam")
    n_beam = lax.axis_size("beam")
    h = lax.rem(ap, 2)
    t = lax.rem(ap // 2, 2)
    up = (ap, lax.rem(z + 1, n_beam))
    down = (ap, lax.rem(z + n_beam - 1, n_beam))
    core = (ap + 1 - 2 * h, z)
    across = (ap + 2 - 4 * t, z)
    first = z == 0
    last = z == n_beam - 1
    beams = x.shape[1]
    blocks0 = beams // BLK
    parts = [(1 - h) * 2 + 1 - t, h * 2 + 1 - t, (1 - h) * 2 + t, h * 2 + t]

    r0 = (r0a, r0b, r0c, r0d)
    l1 = (l1a, l1b)

    loads = [pltpu.make_async_copy(sub.at[0], x, in_sem.at[0])]
    loads[0].start()
    kloads = []
    for i in range(4):
        cols = pl.ds(pl.multiple_of(parts[i] * Q, Q), Q)
        for c in range(2):
            cp = pltpu.make_async_copy(kern.at[0, c, :, cols], kc.at[i, :, pl.ds(c * Q, Q)], k_sem.at[2 * i + c])
            cp.start()
            kloads.append(cp)
    for k, (src, dst) in enumerate(((w0h, w0t), (w1h, w1t))):
        cp = pltpu.make_async_copy(src.at[0], dst, in_sem.at[1 + k])
        cp.start()
        loads.append(cp)

    barrier = pltpu.get_barrier_semaphore()
    peers = [(ap, lax.rem(z + k, n_beam)) for k in range(1, n_beam)] + [core, across]
    for peer in peers:
        pl.semaphore_signal(barrier, inc=1, device_id=peer, device_id_type=MESH)

    def send(src, dst, ssem, rsem, peer):
        cp = pltpu.make_async_remote_copy(src, dst, ssem, rsem, device_id=peer, device_id_type=MESH)
        cp.start()
        return cp

    def rims(buf, i, blocks, ssem, rsem):
        low = send(buf[i].at[pl.ds(RIM_BLK, RIM_BLK)], buf[i].at[pl.ds(RIM_BLK + blocks, RIM_BLK)], ssem.at[i, 0], rsem.at[i, 0], down)
        high = send(buf[i].at[pl.ds(blocks, RIM_BLK)], buf[i].at[pl.ds(0, RIM_BLK)], ssem.at[i, 1], rsem.at[i, 1], up)
        return [low, high]

    def clear_ends(buf, i, blocks):
        @pl.when(first)
        def _():
            buf[i][pl.ds(0, RIM_BLK)] = jnp.zeros((RIM_BLK, BLK, 2 * Q), BF16)

        @pl.when(last)
        def _():
            buf[i][pl.ds(RIM_BLK + blocks, RIM_BLK)] = jnp.zeros((RIM_BLK, BLK, 2 * Q), BF16)

    r_cps = []
    loads[0].wait()
    for i in range(4):
        kloads[2 * i].wait()
        kloads[2 * i + 1].wait()
        re, im = complex_product(x[...].reshape(2 * beams, x.shape[2]), kc[i], beams)
        r0[i][pl.ds(RIM_BLK, blocks0), :, pl.ds(0, Q)] = re.astype(BF16).reshape(blocks0, BLK, Q)
        r0[i][pl.ds(RIM_BLK, blocks0), :, pl.ds(Q, Q)] = im.astype(BF16).reshape(blocks0, BLK, Q)
        if i == 0:
            pl.semaphore_wait(barrier, len(peers))
            o_cp = send(own, other, o_ssem, o_rsem, across)
        r_cps.append(rims(r0, i, blocks0, r_ssem, r_rsem))

    order = [n_beam // 2]
    for k in range(n_beam // 2 - 1, 0, -1):
        order += [k, n_beam - k]
    order.append(0)
    n_own = own.shape[0]

    def places(row):
        table = []
        for k in order:
            d = lax.rem(z + k, n_beam)
            one = two = jnp.int32(n_own)
            for o in reversed(range(n_own)):
                hit = row[o] == d
                two = jnp.where(hit, one, two)
                one = jnp.where(hit, jnp.int32(o), one)
            table.append((one, two))
        return table

    own_places = places(own)
    o_cp.wait_recv()
    across_places = places(other)
    for buf in (px, yo):
        buf[n_own] = jnp.zeros((OS, 2 * Q), BF16)

    def window(starts, j, blocks):
        at = starts[j, ap] - (blocks * z - RIM_BLK)
        return jnp.minimum(jnp.maximum(at, 2 * j), 2 * j + 4)

    def turn(src, dst, lo, hi):
        for j in range(lo, hi):
            for c in range(2):
                dst[j, c] = src[j, c].T

    n0 = w0.shape[0]
    n1 = w1.shape[0]
    loads[1].wait()
    turn(w0t, w0, 0, n0)
    loads[2].wait()
    blocks1 = n0 * PS // BLK
    q_cps = []
    l_cps = []
    for i in range(4):
        r_cps[i][0].wait_recv()
        r_cps[i][1].wait_recv()
        clear_ends(r0, i, blocks0)
        u = i // 2
        if i % 2:
            q_cps[u].wait_recv()
        for j in range(n0):
            at = window(st0, j, blocks0)
            re, im = complex_product(w0[j].reshape(2 * PS, WIN), r0[i][pl.ds(at, NW)].reshape(WIN, 2 * Q), PS)
            rows = pl.ds(j * PS, PS)
            if i % 2 == 0:
                s0[u, rows, pl.ds(0, Q)] = re.astype(BF16)
                s0[u, rows, pl.ds(Q, Q)] = im.astype(BF16)
            else:
                to = pl.ds(RIM_BLK + j * PS // BLK, PS // BLK)
                for part, lanes in ((re, pl.ds(0, Q)), (im, pl.ds(Q, Q))):
                    both = part.astype(BF16).astype(F32) + q0[u, rows, lanes].astype(F32)
                    l1[u][to, :, lanes] = both.astype(BF16).reshape(PS // BLK, BLK, Q)
        if i % 2 == 0:
            q_cps.append(send(s0.at[u], q0.at[u], q_ssem.at[u], q_rsem.at[u], core))
        else:
            l_cps.append(rims(l1, u, blocks1, l_ssem, l_rsem))
        if i < 2:
            turn(w1t, w1, i * n1 // 2, (i + 1) * n1 // 2)

    x_cps = []
    for u in range(2):
        l_cps[u][0].wait_recv()
        l_cps[u][1].wait_recv()
        clear_ends(l1, u, blocks1)
        dst = yo if u else px
        for j in range(n1):
            at = window(st1, j, blocks1)
            re, im = complex_product(w1[j].reshape(2 * PS, WIN), l1[u][pl.ds(at, NW)].reshape(WIN, 2 * Q), PS)
            sectors = pl.ds(j * PS // OS, PS // OS)
            dst[sectors, :, pl.ds(0, Q)] = re.astype(BF16).reshape(PS // OS, OS, Q)
            dst[sectors, :, pl.ds(Q, Q)] = im.astype(BF16).reshape(PS // OS, OS, Q)
        if u == 0:
            for n in range(n_beam):
                for c in range(2):
                    sx[n, c] = px[across_places[n][c]]
                x_cps.append(send(sx.at[n], rx.at[n], x_ssem.at[n], x_rsem.at[n], across))

    mine = pl.ds(2 * z, 2)
    a_cps = []
    for n, k in enumerate(order):
        d = lax.rem(z + k, n_beam)
        x_cps[n].wait_recv()
        for c in range(2):
            sector = (yo[own_places[n][c]].astype(F32) + rx[n, c].astype(F32)).astype(BF16)
            og[2 * d + c, 0] = sector[:, :Q]
            og[2 * d + c, 1] = sector[:, Q:]
        if k:
            a_cps.append(send(og.at[pl.ds(2 * d, 2)], out.at[mine], a_ssem.at[n], a_rsem.at[n], (ap, d)))
    local = pltpu.make_async_copy(og.at[mine], out.at[mine], o_sem)
    local.start()
    local.wait()
    for cp in a_cps:
        cp.wait()
    o_cp.wait_send()
    for cp in [c for pair in r_cps + l_cps for c in pair] + q_cps + x_cps:
        cp.wait_send()


def local(subimages, range_kernel, weights0, starts0, weights1, starts1, owners):
    beams, rng = subimages.shape[2], subimages.shape[3]
    n0, n1 = weights0.shape[1], weights1.shape[1]
    n_own = owners.shape[1]
    n_beam = lax.axis_size("beam")
    slots = 2 * n_beam
    hbm = pl.BlockSpec(memory_space=pl.ANY)
    smem = pl.BlockSpec(memory_space=pltpu.SMEM)
    dma = pltpu.SemaphoreType.DMA
    merged = pl.pallas_call(
        kernel,
        out_shape=jax.ShapeDtypeStruct((slots, 2, OS, Q), BF16),
        in_specs=[hbm, hbm, hbm, hbm, smem, smem, smem],
        out_specs=pl.BlockSpec(memory_space=pltpu.VMEM),
        scratch_shapes=[
            pltpu.VMEM((2, beams, rng), BF16),
            pltpu.VMEM((4, rng, 2 * Q), BF16),
            pltpu.VMEM((n0, 2, WIN, PS), BF16),
            pltpu.VMEM((n1, 2, WIN, PS), BF16),
            pltpu.VMEM((n0, 2, PS, WIN), BF16),
            pltpu.VMEM((n1, 2, PS, WIN), BF16),
            pltpu.VMEM((beams // BLK + 2 * RIM_BLK, BLK, 2 * Q), BF16),
            pltpu.VMEM((beams // BLK + 2 * RIM_BLK, BLK, 2 * Q), BF16),
            pltpu.VMEM((beams // BLK + 2 * RIM_BLK, BLK, 2 * Q), BF16),
            pltpu.VMEM((beams // BLK + 2 * RIM_BLK, BLK, 2 * Q), BF16),
            pltpu.VMEM((2, n0 * PS, 2 * Q), BF16),
            pltpu.VMEM((2, n0 * PS, 2 * Q), BF16),
            pltpu.VMEM((n0 * PS // BLK + 2 * RIM_BLK, BLK, 2 * Q), BF16),
            pltpu.VMEM((n0 * PS // BLK + 2 * RIM_BLK, BLK, 2 * Q), BF16),
            pltpu.VMEM((n_beam, 2, OS, 2 * Q), BF16),
            pltpu.VMEM((n_beam, 2, OS, 2 * Q), BF16),
            pltpu.VMEM((n_own + 1, OS, 2 * Q), BF16),
            pltpu.VMEM((n_own + 1, OS, 2 * Q), BF16),
            pltpu.VMEM((slots, 2, OS, Q), BF16),
            pltpu.SMEM((n_own,), jnp.int32),
            dma((3,)),
            dma((8,)),
            dma((4, 2)),
            dma((4, 2)),
            dma((2,)),
            dma((2,)),
            dma((2, 2)),
            dma((2, 2)),
            dma((n_beam,)),
            dma((n_beam,)),
            dma((n_beam - 1,)),
            dma((n_beam - 1,)),
            dma,
            dma,
            dma,
        ],
        compiler_params=pltpu.CompilerParams(collective_id=0, has_side_effects=True),
    )(
        subimages,
        range_kernel,
        jnp.swapaxes(weights0, 3, 4),
        jnp.swapaxes(weights1, 3, 4),
        starts0.T,
        starts1.T,
        owners.reshape(n_own),
    )
    return merged[None]


def solution(mesh):
    return jax.shard_map(
        local,
        mesh=mesh,
        in_specs=(
            P("aperture", None, "beam", None),
            P("aperture", None, None, None),
            P("aperture", "beam", None, None, None),
            P(None, "beam"),
            P("aperture", "beam", None, None, None),
            P(None, "beam"),
            P("aperture", "beam", None),
        ),
        out_specs=P("aperture", "beam", None, None, None),
        check_vma=False,
    )
```

```python
import jax
import jax.numpy as jnp
from jax import lax
from jax.experimental import pallas as pl
from jax.experimental.pallas import tpu as pltpu
from jax.sharding import PartitionSpec as P

BLK = 32
WIN = 320
PS = 128
OS = 64
NW = 10
RIM_BLK = 6
Q = 128
MESH = pl.DeviceIdType.MESH
BF16 = jnp.bfloat16
F32 = jnp.float32


def complex_product(left, right, rows):
    p = jnp.dot(left, right, preferred_element_type=F32)
    return p[:rows, :Q] - p[rows:, Q:], p[:rows, Q:] + p[rows:, :Q]


def kernel(
    sub, kern, w0h, w1h, st0h, st1h, ownh, out,
    x, kc, w0t, w1t, w0, w1, r0a, r0b, r0c, r0d, s0, q0, l1a, l1b, sx, rx, px, yo, og, st0, st1, own, other,
    in_sem, k_sem, r_ssem, r_rsem, q_ssem, q_rsem, l_ssem, l_rsem, x_ssem, x_rsem, a_ssem, a_rsem, o_sem, o_ssem, o_rsem, ring_sem,
):
    ap = lax.axis_index("aperture")
    z = lax.axis_index("beam")
    n_beam = lax.axis_size("beam")
    h = lax.rem(ap, 2)
    t = lax.rem(ap // 2, 2)
    up = (ap, lax.rem(z + 1, n_beam))
    down = (ap, lax.rem(z + n_beam - 1, n_beam))
    core = (ap + 1 - 2 * h, z)
    across = (ap + 2 - 4 * t, z)
    first = z == 0
    last = z == n_beam - 1
    beams = x.shape[1]
    blocks0 = beams // BLK
    parts = [(1 - h) * 2 + 1 - t, h * 2 + 1 - t, (1 - h) * 2 + t, h * 2 + t]

    r0 = (r0a, r0b, r0c, r0d)
    l1 = (l1a, l1b)

    barrier = pltpu.get_barrier_semaphore()
    peers = [down, up, core, across]
    for peer in peers:
        pl.semaphore_signal(barrier, inc=1, device_id=peer, device_id_type=MESH)

    loads = [pltpu.make_async_copy(sub.at[0], x, in_sem.at[0])]
    loads[0].start()
    kloads = []
    for i in range(4):
        cols = pl.ds(pl.multiple_of(parts[i] * Q, Q), Q)
        for c in range(2):
            cp = pltpu.make_async_copy(kern.at[0, c, :, cols], kc.at[i, :, pl.ds(c * Q, Q)], k_sem.at[2 * i + c])
            kloads.append(cp)
    for cp in kloads[:2]:
        cp.start()
    for k, (src, dst) in enumerate(((w0h, w0t), (w1h, w1t))):
        loads.append(pltpu.make_async_copy(src.at[0], dst, in_sem.at[1 + k]))
    tables = []
    for k, (src, dst) in enumerate(((ownh, own), (st0h, st0), (st1h, st1))):
        tables.append(pltpu.make_async_copy(src, dst, in_sem.at[3 + k]))
        tables[k].start()

    def announce(r):
        for k in (1 << r, n_beam - (1 << r)):
            pl.semaphore_signal(ring_sem.at[r], inc=1, device_id=(ap, lax.rem(z + k, n_beam)), device_id_type=MESH)

    def send(src, dst, ssem, rsem, peer):
        cp = pltpu.make_async_remote_copy(src, dst, ssem, rsem, device_id=peer, device_id_type=MESH)
        cp.start()
        return cp

    def rims(buf, i, blocks, ssem, rsem):
        low = send(buf[i].at[pl.ds(RIM_BLK, RIM_BLK)], buf[i].at[pl.ds(RIM_BLK + blocks, RIM_BLK)], ssem.at[i, 0], rsem.at[i, 0], down)
        high = send(buf[i].at[pl.ds(blocks, RIM_BLK)], buf[i].at[pl.ds(0, RIM_BLK)], ssem.at[i, 1], rsem.at[i, 1], up)
        return [low, high]

    def clear_ends(buf, i, blocks):
        @pl.when(first)
        def _():
            buf[i][pl.ds(0, RIM_BLK)] = jnp.zeros((RIM_BLK, BLK, 2 * Q), BF16)

        @pl.when(last)
        def _():
            buf[i][pl.ds(RIM_BLK + blocks, RIM_BLK)] = jnp.zeros((RIM_BLK, BLK, 2 * Q), BF16)

    r_cps = []
    loads[0].wait()
    for i in range(4):
        kloads[2 * i].wait()
        kloads[2 * i + 1].wait()
        if i == 0:
            for cp in kloads[2:] + loads[1:]:
                cp.start()
        re, im = complex_product(x[...].reshape(2 * beams, x.shape[2]), kc[i], beams)
        r0[i][pl.ds(RIM_BLK, blocks0), :, pl.ds(0, Q)] = re.astype(BF16).reshape(blocks0, BLK, Q)
        r0[i][pl.ds(RIM_BLK, blocks0), :, pl.ds(Q, Q)] = im.astype(BF16).reshape(blocks0, BLK, Q)
        if i == 0:
            pl.semaphore_wait(barrier, len(peers))
            announce(0)
            o_cp = send(ownh, other, o_ssem, o_rsem, across)
        r_cps.append(rims(r0, i, blocks0, r_ssem, r_rsem))

    order = [n_beam // 2]
    for k in range(n_beam // 2 - 1, 0, -1):
        order += [k, n_beam - k]
    order.append(0)
    n_own = own.shape[0]

    def places(row):
        table = []
        for k in order:
            d = lax.rem(z + k, n_beam)
            one = two = jnp.int32(n_own)
            for o in reversed(range(n_own)):
                hit = row[o] == d
                two = jnp.where(hit, one, two)
                one = jnp.where(hit, jnp.int32(o), one)
            table.append((one, two))
        return table

    for cp in tables:
        cp.wait()
    own_places = places(own)
    o_cp.wait_recv()
    across_places = places(other)
    for buf in (px, yo):
        buf[n_own] = jnp.zeros((OS, 2 * Q), BF16)

    def window(starts, j, blocks):
        at = starts[j, ap] - (blocks * z - RIM_BLK)
        return jnp.minimum(jnp.maximum(at, 2 * j), 2 * j + 4)

    def turn(src, dst, lo, hi):
        for j in range(lo, hi):
            for c in range(2):
                dst[j, c] = src[j, c].T

    n0 = w0.shape[0]
    n1 = w1.shape[0]
    loads[1].wait()
    turn(w0t, w0, 0, n0)
    loads[2].wait()
    blocks1 = n0 * PS // BLK
    q_cps = []
    l_cps = []
    for i in range(4):
        r_cps[i][0].wait_recv()
        r_cps[i][1].wait_recv()
        clear_ends(r0, i, blocks0)
        u = i // 2
        if i % 2:
            q_cps[u].wait_recv()
        for j in range(n0):
            at = window(st0, j, blocks0)
            re, im = complex_product(w0[j].reshape(2 * PS, WIN), r0[i][pl.ds(at, NW)].reshape(WIN, 2 * Q), PS)
            rows = pl.ds(j * PS, PS)
            if i % 2 == 0:
                s0[u, rows, pl.ds(0, Q)] = re.astype(BF16)
                s0[u, rows, pl.ds(Q, Q)] = im.astype(BF16)
            else:
                to = pl.ds(RIM_BLK + j * PS // BLK, PS // BLK)
                for part, lanes in ((re, pl.ds(0, Q)), (im, pl.ds(Q, Q))):
                    both = part.astype(BF16).astype(F32) + q0[u, rows, lanes].astype(F32)
                    l1[u][to, :, lanes] = both.astype(BF16).reshape(PS // BLK, BLK, Q)
        if i % 2 == 0:
            q_cps.append(send(s0.at[u], q0.at[u], q_ssem.at[u], q_rsem.at[u], core))
        else:
            l_cps.append(rims(l1, u, blocks1, l_ssem, l_rsem))
        if i < 2:
            pl.semaphore_wait(ring_sem.at[i], 2)
            announce(i + 1)
            turn(w1t, w1, i * n1 // 2, (i + 1) * n1 // 2)

    x_cps = []
    for u in range(2):
        l_cps[u][0].wait_recv()
        l_cps[u][1].wait_recv()
        clear_ends(l1, u, blocks1)
        dst = yo if u else px
        for j in range(n1):
            at = window(st1, j, blocks1)
            re, im = complex_product(w1[j].reshape(2 * PS, WIN), l1[u][pl.ds(at, NW)].reshape(WIN, 2 * Q), PS)
            sectors = pl.ds(j * PS // OS, PS // OS)
            dst[sectors, :, pl.ds(0, Q)] = re.astype(BF16).reshape(PS // OS, OS, Q)
            dst[sectors, :, pl.ds(Q, Q)] = im.astype(BF16).reshape(PS // OS, OS, Q)
        if u == 0:
            for n in range(n_beam):
                for c in range(2):
                    sx[n, c] = px[across_places[n][c]]
                x_cps.append(send(sx.at[n], rx.at[n], x_ssem.at[n], x_rsem.at[n], across))

    pl.semaphore_wait(ring_sem.at[2], 2)

    mine = pl.ds(2 * z, 2)
    a_cps = []
    for n, k in enumerate(order):
        d = lax.rem(z + k, n_beam)
        x_cps[n].wait_recv()
        for c in range(2):
            sector = (yo[own_places[n][c]].astype(F32) + rx[n, c].astype(F32)).astype(BF16)
            og[2 * d + c, 0] = sector[:, :Q]
            og[2 * d + c, 1] = sector[:, Q:]
        if k:
            a_cps.append(send(og.at[pl.ds(2 * d, 2)], out.at[mine], a_ssem.at[n], a_rsem.at[n], (ap, d)))
    local = pltpu.make_async_copy(og.at[mine], out.at[mine], o_sem)
    local.start()
    local.wait()
    for cp in a_cps:
        cp.wait()
    o_cp.wait_send()
    for cp in [c for pair in r_cps + l_cps for c in pair] + q_cps + x_cps:
        cp.wait_send()


def local(subimages, range_kernel, weights0, starts0, weights1, starts1, owners):
    beams, rng = subimages.shape[2], subimages.shape[3]
    n0, n1 = weights0.shape[1], weights1.shape[1]
    n_own = owners.shape[1]
    n_beam = lax.axis_size("beam")
    slots = 2 * n_beam
    hbm = pl.BlockSpec(memory_space=pl.ANY)
    dma = pltpu.SemaphoreType.DMA
    merged = pl.pallas_call(
        kernel,
        out_shape=pltpu.VMEM((slots, 2, OS, Q), BF16),
        in_specs=[hbm] * 7,
        out_specs=pl.BlockSpec(memory_space=pltpu.VMEM),
        scratch_shapes=[
            pltpu.VMEM((2, beams, rng), BF16),
            pltpu.VMEM((4, rng, 2 * Q), BF16),
            pltpu.VMEM((n0, 2, WIN, PS), BF16),
            pltpu.VMEM((n1, 2, WIN, PS), BF16),
            pltpu.VMEM((n0, 2, PS, WIN), BF16),
            pltpu.VMEM((n1, 2, PS, WIN), BF16),
            pltpu.VMEM((beams // BLK + 2 * RIM_BLK, BLK, 2 * Q), BF16),
            pltpu.VMEM((beams // BLK + 2 * RIM_BLK, BLK, 2 * Q), BF16),
            pltpu.VMEM((beams // BLK + 2 * RIM_BLK, BLK, 2 * Q), BF16),
            pltpu.VMEM((beams // BLK + 2 * RIM_BLK, BLK, 2 * Q), BF16),
            pltpu.VMEM((2, n0 * PS, 2 * Q), BF16),
            pltpu.VMEM((2, n0 * PS, 2 * Q), BF16),
            pltpu.VMEM((n0 * PS // BLK + 2 * RIM_BLK, BLK, 2 * Q), BF16),
            pltpu.VMEM((n0 * PS // BLK + 2 * RIM_BLK, BLK, 2 * Q), BF16),
            pltpu.VMEM((n_beam, 2, OS, 2 * Q), BF16),
            pltpu.VMEM((n_beam, 2, OS, 2 * Q), BF16),
            pltpu.VMEM((n_own + 1, OS, 2 * Q), BF16),
            pltpu.VMEM((n_own + 1, OS, 2 * Q), BF16),
            pltpu.VMEM((slots, 2, OS, Q), BF16),
            pltpu.SMEM(starts0.shape[::-1], jnp.int32),
            pltpu.SMEM(starts1.shape[::-1], jnp.int32),
            pltpu.SMEM((n_own,), jnp.int32),
            pltpu.SMEM((n_own,), jnp.int32),
            dma((6,)),
            dma((8,)),
            dma((4, 2)),
            dma((4, 2)),
            dma((2,)),
            dma((2,)),
            dma((2, 2)),
            dma((2, 2)),
            dma((n_beam,)),
            dma((n_beam,)),
            dma((n_beam - 1,)),
            dma((n_beam - 1,)),
            dma,
            dma,
            dma,
            pltpu.SemaphoreType.REGULAR((3,)),
        ],
        compiler_params=pltpu.CompilerParams(collective_id=0, has_side_effects=True),
    )(
        subimages,
        range_kernel,
        jnp.swapaxes(weights0, 3, 4),
        jnp.swapaxes(weights1, 3, 4),
        starts0.T,
        starts1.T,
        owners.reshape(n_own),
    )
    return merged[None]


def solution(mesh):
    return jax.shard_map(
        local,
        mesh=mesh,
        in_specs=(
            P("aperture", None, "beam", None),
            P("aperture", None, None, None),
            P("aperture", "beam", None, None, None),
            P(None, "beam"),
            P("aperture", "beam", None, None, None),
            P(None, "beam"),
            P("aperture", "beam", None),
        ),
        out_specs=P("aperture", "beam", None, None, None),
        check_vma=False,
    )
```

```python
import jax
import jax.numpy as jnp
from jax import lax
from jax.experimental import pallas as pl
from jax.experimental.pallas import tpu as pltpu
from jax.sharding import PartitionSpec as P

BLK = 32
WIN = 320
PS = 128
OS = 64
NW = 10
RIM_BLK = 6
Q = 128
MESH = pl.DeviceIdType.MESH
BF16 = jnp.bfloat16
F32 = jnp.float32


def complex_product(left, right, rows):
    p = jnp.dot(left, right, preferred_element_type=F32)
    return p[:rows, :Q] - p[rows:, Q:], p[:rows, Q:] + p[rows:, :Q]


def kernel(
    sub, kern, w0h, w1h, st0h, st1h, ownh, out,
    x, kc, w0t, w1t, w0, w1, r0a, r0b, r0c, r0d, s0, q0, l1a, l1b, sx, rx, px, yo, og, st0, st1, own, other,
    in_sem, k_sem, r_ssem, r_rsem, q_ssem, q_rsem, l_ssem, l_rsem, x_ssem, x_rsem, a_ssem, a_rsem, o_sem, o_ssem, o_rsem, ring_sem,
):
    ap = lax.axis_index("aperture")
    z = lax.axis_index("beam")
    n_beam = lax.axis_size("beam")
    h = lax.rem(ap, 2)
    t = lax.rem(ap // 2, 2)
    up = (ap, lax.rem(z + 1, n_beam))
    down = (ap, lax.rem(z + n_beam - 1, n_beam))
    core = (ap + 1 - 2 * h, z)
    across = (ap + 2 - 4 * t, z)
    first = z == 0
    last = z == n_beam - 1
    below = z > 0
    above = z < n_beam - 1
    beams = x.shape[1]
    blocks0 = beams // BLK
    parts = [(1 - h) * 2 + 1 - t, h * 2 + 1 - t, (1 - h) * 2 + t, h * 2 + t]

    r0 = (r0a, r0b, r0c, r0d)
    l1 = (l1a, l1b)

    barrier = pltpu.get_barrier_semaphore()

    def signal(sem, peer):
        pl.semaphore_signal(sem, inc=1, device_id=peer, device_id_type=MESH)

    def pair(k, act):
        pl.when(z + k < n_beam)(lambda: act((ap, lax.rem(z + k, n_beam))))
        pl.when(z >= k)(lambda: act((ap, lax.rem(z + n_beam - k, n_beam))))

    def pair_count(k):
        return jnp.where(z + k < n_beam, 1, 0) + jnp.where(z >= k, 1, 0)

    signal(barrier, core)
    signal(barrier, across)
    pair(1, lambda peer: signal(barrier, peer))

    loads = [pltpu.make_async_copy(sub.at[0], x, in_sem.at[0])]
    loads[0].start()
    kloads = []
    for i in range(4):
        cols = pl.ds(pl.multiple_of(parts[i] * Q, Q), Q)
        for c in range(2):
            cp = pltpu.make_async_copy(kern.at[0, c, :, cols], kc.at[i, :, pl.ds(c * Q, Q)], k_sem.at[2 * i + c])
            kloads.append(cp)
    for cp in kloads[:2]:
        cp.start()
    for k, (src, dst) in enumerate(((w0h, w0t), (w1h, w1t))):
        loads.append(pltpu.make_async_copy(src.at[0], dst, in_sem.at[1 + k]))
    tables = []
    for k, (src, dst) in enumerate(((ownh, own), (st0h, st0), (st1h, st1))):
        tables.append(pltpu.make_async_copy(src, dst, in_sem.at[3 + k]))
        tables[k].start()

    def announce(r):
        pair(1 << r, lambda peer: signal(ring_sem.at[r], peer))

    def heard(r):
        pl.semaphore_wait(ring_sem.at[r], pair_count(1 << r))

    def send(src, dst, ssem, rsem, peer):
        cp = pltpu.make_async_remote_copy(src, dst, ssem, rsem, device_id=peer, device_id_type=MESH)
        cp.start()
        return cp

    def rims(buf, i, blocks, ssem, rsem):
        def copy(src, dst, side, peer):
            return pltpu.make_async_remote_copy(
                buf[i].at[pl.ds(src, RIM_BLK)],
                buf[i].at[pl.ds(dst, RIM_BLK)],
                ssem.at[i, side],
                rsem.at[i, side],
                device_id=peer,
                device_id_type=MESH,
            )

        low = copy(RIM_BLK, RIM_BLK + blocks, 0, down)
        high = copy(blocks, 0, 1, up)
        pl.when(below)(low.start)
        pl.when(above)(high.start)
        return low, high

    def rims_in(cps):
        pl.when(above)(cps[0].wait_recv)
        pl.when(below)(cps[1].wait_recv)

    def rims_out(cps):
        pl.when(below)(cps[0].wait_send)
        pl.when(above)(cps[1].wait_send)

    def clear_ends(buf, i, blocks):
        @pl.when(first)
        def _():
            buf[i][pl.ds(0, RIM_BLK)] = jnp.zeros((RIM_BLK, BLK, 2 * Q), BF16)

        @pl.when(last)
        def _():
            buf[i][pl.ds(RIM_BLK + blocks, RIM_BLK)] = jnp.zeros((RIM_BLK, BLK, 2 * Q), BF16)

    r_cps = []
    loads[0].wait()
    for i in range(4):
        kloads[2 * i].wait()
        kloads[2 * i + 1].wait()
        if i == 0:
            for cp in kloads[2:] + loads[1:]:
                cp.start()
        re, im = complex_product(x[...].reshape(2 * beams, x.shape[2]), kc[i], beams)
        r0[i][pl.ds(RIM_BLK, blocks0), :, pl.ds(0, Q)] = re.astype(BF16).reshape(blocks0, BLK, Q)
        r0[i][pl.ds(RIM_BLK, blocks0), :, pl.ds(Q, Q)] = im.astype(BF16).reshape(blocks0, BLK, Q)
        if i == 0:
            pl.semaphore_wait(barrier, 2 + pair_count(1))
            announce(0)
            o_cp = send(ownh, other, o_ssem, o_rsem, across)
        r_cps.append(rims(r0, i, blocks0, r_ssem, r_rsem))
        if i == 2:
            heard(0)
            announce(1)
    heard(1)
    announce(2)

    order = [n_beam // 2]
    for k in range(n_beam // 2 - 1, 0, -1):
        order += [k, n_beam - k]
    order.append(0)
    n_own = own.shape[0]

    def places(row):
        table = []
        for k in order:
            d = lax.rem(z + k, n_beam)
            one = two = jnp.int32(n_own)
            for o in reversed(range(n_own)):
                hit = row[o] == d
                two = jnp.where(hit, one, two)
                one = jnp.where(hit, jnp.int32(o), one)
            table.append((one, two))
        return table

    for cp in tables:
        cp.wait()
    own_places = places(own)
    o_cp.wait_recv()
    across_places = places(other)
    for buf in (px, yo):
        buf[n_own] = jnp.zeros((OS, 2 * Q), BF16)

    def window(starts, j, blocks):
        at = starts[j, ap] - (blocks * z - RIM_BLK)
        return jnp.minimum(jnp.maximum(at, 2 * j), 2 * j + 4)

    def turn(src, dst, lo, hi):
        for j in range(lo, hi):
            for c in range(2):
                dst[j, c] = src[j, c].T

    n0 = w0.shape[0]
    n1 = w1.shape[0]
    loads[1].wait()
    turn(w0t, w0, 0, n0)
    loads[2].wait()
    blocks1 = n0 * PS // BLK
    q_cps = []
    l_cps = []
    for i in range(4):
        rims_in(r_cps[i])
        clear_ends(r0, i, blocks0)
        u = i // 2
        if i % 2:
            q_cps[u].wait_recv()
        for j in range(n0):
            at = window(st0, j, blocks0)
            re, im = complex_product(w0[j].reshape(2 * PS, WIN), r0[i][pl.ds(at, NW)].reshape(WIN, 2 * Q), PS)
            rows = pl.ds(j * PS, PS)
            if i % 2 == 0:
                s0[u, rows, pl.ds(0, Q)] = re.astype(BF16)
                s0[u, rows, pl.ds(Q, Q)] = im.astype(BF16)
            else:
                to = pl.ds(RIM_BLK + j * PS // BLK, PS // BLK)
                for part, lanes in ((re, pl.ds(0, Q)), (im, pl.ds(Q, Q))):
                    both = part.astype(BF16).astype(F32) + q0[u, rows, lanes].astype(F32)
                    l1[u][to, :, lanes] = both.astype(BF16).reshape(PS // BLK, BLK, Q)
        if i % 2 == 0:
            q_cps.append(send(s0.at[u], q0.at[u], q_ssem.at[u], q_rsem.at[u], core))
        else:
            l_cps.append(rims(l1, u, blocks1, l_ssem, l_rsem))
        if i < 2:
            if i == 0:
                heard(2)
                announce(3)
            turn(w1t, w1, i * n1 // 2, (i + 1) * n1 // 2)

    x_cps = []
    for u in range(2):
        rims_in(l_cps[u])
        clear_ends(l1, u, blocks1)
        dst = yo if u else px
        for j in range(n1):
            at = window(st1, j, blocks1)
            re, im = complex_product(w1[j].reshape(2 * PS, WIN), l1[u][pl.ds(at, NW)].reshape(WIN, 2 * Q), PS)
            sectors = pl.ds(j * PS // OS, PS // OS)
            dst[sectors, :, pl.ds(0, Q)] = re.astype(BF16).reshape(PS // OS, OS, Q)
            dst[sectors, :, pl.ds(Q, Q)] = im.astype(BF16).reshape(PS // OS, OS, Q)
        if u == 0:
            for n in range(n_beam):
                for c in range(2):
                    sx[n, c] = px[across_places[n][c]]
                x_cps.append(send(sx.at[n], rx.at[n], x_ssem.at[n], x_rsem.at[n], across))

    heard(3)

    mine = pl.ds(2 * z, 2)
    a_cps = []
    for n, k in enumerate(order):
        d = lax.rem(z + k, n_beam)
        x_cps[n].wait_recv()
        for c in range(2):
            sector = (yo[own_places[n][c]].astype(F32) + rx[n, c].astype(F32)).astype(BF16)
            og[2 * d + c, 0] = sector[:, :Q]
            og[2 * d + c, 1] = sector[:, Q:]
        if k:
            a_cps.append(send(og.at[pl.ds(2 * d, 2)], out.at[mine], a_ssem.at[n], a_rsem.at[n], (ap, d)))
    local = pltpu.make_async_copy(og.at[mine], out.at[mine], o_sem)
    local.start()
    local.wait()
    for cp in a_cps:
        cp.wait()
    o_cp.wait_send()
    for cps in r_cps + l_cps:
        rims_out(cps)
    for cp in q_cps + x_cps:
        cp.wait_send()


def local(subimages, range_kernel, weights0, starts0, weights1, starts1, owners):
    beams, rng = subimages.shape[2], subimages.shape[3]
    n0, n1 = weights0.shape[1], weights1.shape[1]
    n_own = owners.shape[1]
    n_beam = lax.axis_size("beam")
    slots = 2 * n_beam
    hbm = pl.BlockSpec(memory_space=pl.ANY)
    dma = pltpu.SemaphoreType.DMA
    merged = pl.pallas_call(
        kernel,
        out_shape=pltpu.VMEM((slots, 2, OS, Q), BF16),
        in_specs=[hbm] * 7,
        out_specs=pl.BlockSpec(memory_space=pltpu.VMEM),
        scratch_shapes=[
            pltpu.VMEM((2, beams, rng), BF16),
            pltpu.VMEM((4, rng, 2 * Q), BF16),
            pltpu.VMEM((n0, 2, WIN, PS), BF16),
            pltpu.VMEM((n1, 2, WIN, PS), BF16),
            pltpu.VMEM((n0, 2, PS, WIN), BF16),
            pltpu.VMEM((n1, 2, PS, WIN), BF16),
            pltpu.VMEM((beams // BLK + 2 * RIM_BLK, BLK, 2 * Q), BF16),
            pltpu.VMEM((beams // BLK + 2 * RIM_BLK, BLK, 2 * Q), BF16),
            pltpu.VMEM((beams // BLK + 2 * RIM_BLK, BLK, 2 * Q), BF16),
            pltpu.VMEM((beams // BLK + 2 * RIM_BLK, BLK, 2 * Q), BF16),
            pltpu.VMEM((2, n0 * PS, 2 * Q), BF16),
            pltpu.VMEM((2, n0 * PS, 2 * Q), BF16),
            pltpu.VMEM((n0 * PS // BLK + 2 * RIM_BLK, BLK, 2 * Q), BF16),
            pltpu.VMEM((n0 * PS // BLK + 2 * RIM_BLK, BLK, 2 * Q), BF16),
            pltpu.VMEM((n_beam, 2, OS, 2 * Q), BF16),
            pltpu.VMEM((n_beam, 2, OS, 2 * Q), BF16),
            pltpu.VMEM((n_own + 1, OS, 2 * Q), BF16),
            pltpu.VMEM((n_own + 1, OS, 2 * Q), BF16),
            pltpu.VMEM((slots, 2, OS, Q), BF16),
            pltpu.SMEM(starts0.shape[::-1], jnp.int32),
            pltpu.SMEM(starts1.shape[::-1], jnp.int32),
            pltpu.SMEM((n_own,), jnp.int32),
            pltpu.SMEM((n_own,), jnp.int32),
            dma((6,)),
            dma((8,)),
            dma((4, 2)),
            dma((4, 2)),
            dma((2,)),
            dma((2,)),
            dma((2, 2)),
            dma((2, 2)),
            dma((n_beam,)),
            dma((n_beam,)),
            dma((n_beam - 1,)),
            dma((n_beam - 1,)),
            dma,
            dma,
            dma,
            pltpu.SemaphoreType.REGULAR((4,)),
        ],
        compiler_params=pltpu.CompilerParams(collective_id=0, has_side_effects=True),
    )(
        subimages,
        range_kernel,
        jnp.swapaxes(weights0, 3, 4),
        jnp.swapaxes(weights1, 3, 4),
        starts0.T,
        starts1.T,
        owners.reshape(n_own),
    )
    return merged[None]


def solution(mesh):
    return jax.shard_map(
        local,
        mesh=mesh,
        in_specs=(
            P("aperture", None, "beam", None),
            P("aperture", None, None, None),
            P("aperture", "beam", None, None, None),
            P(None, "beam"),
            P("aperture", "beam", None, None, None),
            P(None, "beam"),
            P("aperture", "beam", None),
        ),
        out_specs=P("aperture", "beam", None, None, None),
        check_vma=False,
    )
```

```python
import jax
import jax.numpy as jnp
from jax import lax
from jax.experimental import pallas as pl
from jax.experimental.pallas import tpu as pltpu
from jax.sharding import PartitionSpec as P

BLK = 32
WIN = 320
PS = 128
OS = 64
NW = 10
RIM_BLK = 6
Q = 128
MESH = pl.DeviceIdType.MESH
BF16 = jnp.bfloat16
F32 = jnp.float32


def complex_product(left, right, rows):
    p = jnp.dot(left, right, preferred_element_type=F32)
    return p[:rows, :Q] - p[rows:, Q:], p[:rows, Q:] + p[rows:, :Q]


def kernel(
    sub, kern, w0h, w1h, st0h, st1h, ownh, out,
    x, kc, w0t, w1t, w0, w1, r0a, r0b, r0c, r0d, s0, q0, l1a, l1b, sx, rx, px, yo, og, st0, st1, own, other,
    in_sem, k_sem, r_ssem, r_rsem, q_ssem, q_rsem, l_ssem, l_rsem, x_ssem, x_rsem, a_ssem, a_rsem, o_sem, o_ssem, o_rsem, ring_sem,
):
    ap = lax.axis_index("aperture")
    z = lax.axis_index("beam")
    n_beam = lax.axis_size("beam")
    h = lax.rem(ap, 2)
    t = lax.rem(ap // 2, 2)
    up = (ap, lax.rem(z + 1, n_beam))
    down = (ap, lax.rem(z + n_beam - 1, n_beam))
    core = (ap + 1 - 2 * h, z)
    across = (ap + 2 - 4 * t, z)
    first = z == 0
    last = z == n_beam - 1
    below = z > 0
    above = z < n_beam - 1
    beams = x.shape[1]
    blocks0 = beams // BLK
    parts = [(1 - h) * 2 + 1 - t, h * 2 + 1 - t, (1 - h) * 2 + t, h * 2 + t]

    r0 = (r0a, r0b, r0c, r0d)
    l1 = (l1a, l1b)

    barrier = pltpu.get_barrier_semaphore()

    def signal(sem, peer):
        pl.semaphore_signal(sem, inc=1, device_id=peer, device_id_type=MESH)

    def pair(k, act):
        pl.when(z + k < n_beam)(lambda: act((ap, lax.rem(z + k, n_beam))))
        pl.when(z >= k)(lambda: act((ap, lax.rem(z + n_beam - k, n_beam))))

    def pair_count(k):
        return jnp.where(z + k < n_beam, 1, 0) + jnp.where(z >= k, 1, 0)

    signal(barrier, core)
    signal(barrier, across)
    pair(1, lambda peer: signal(barrier, peer))

    loads = [pltpu.make_async_copy(sub.at[0], x, in_sem.at[0])]
    loads[0].start()
    kloads = []
    for i in range(4):
        cols = pl.ds(pl.multiple_of(parts[i] * Q, Q), Q)
        for c in range(2):
            cp = pltpu.make_async_copy(kern.at[0, c, :, cols], kc.at[i, :, pl.ds(c * Q, Q)], k_sem.at[2 * i + c])
            kloads.append(cp)
    for cp in kloads[:2]:
        cp.start()
    for k, (src, dst) in enumerate(((w0h, w0t), (w1h, w1t))):
        loads.append(pltpu.make_async_copy(src.at[0], dst, in_sem.at[1 + k]))
    tables = []
    for k, (src, dst) in enumerate(((ownh, own), (st0h, st0), (st1h, st1))):
        tables.append(pltpu.make_async_copy(src, dst, in_sem.at[3 + k]))
        tables[k].start()

    def announce(r):
        pair(1 << r, lambda peer: signal(ring_sem.at[r], peer))

    def heard(r):
        pl.semaphore_wait(ring_sem.at[r], pair_count(1 << r))

    def send(src, dst, ssem, rsem, peer):
        cp = pltpu.make_async_remote_copy(src, dst, ssem, rsem, device_id=peer, device_id_type=MESH)
        cp.start()
        return cp

    def rims(buf, i, blocks, ssem, rsem):
        def copy(src, dst, side, peer):
            return pltpu.make_async_remote_copy(
                buf[i].at[pl.ds(src, RIM_BLK)],
                buf[i].at[pl.ds(dst, RIM_BLK)],
                ssem.at[i, side],
                rsem.at[i, side],
                device_id=peer,
                device_id_type=MESH,
            )

        low = copy(RIM_BLK, RIM_BLK + blocks, 0, down)
        high = copy(blocks, 0, 1, up)
        pl.when(below)(low.start)
        pl.when(above)(high.start)
        return low, high

    def rims_in(cps):
        pl.when(above)(cps[0].wait_recv)
        pl.when(below)(cps[1].wait_recv)

    def rims_out(cps):
        pl.when(below)(cps[0].wait_send)
        pl.when(above)(cps[1].wait_send)

    def clear_ends(buf, i, blocks):
        @pl.when(first)
        def _():
            buf[i][pl.ds(0, RIM_BLK)] = jnp.zeros((RIM_BLK, BLK, 2 * Q), BF16)

        @pl.when(last)
        def _():
            buf[i][pl.ds(RIM_BLK + blocks, RIM_BLK)] = jnp.zeros((RIM_BLK, BLK, 2 * Q), BF16)

    r_cps = []
    loads[0].wait()
    for i in range(4):
        kloads[2 * i].wait()
        kloads[2 * i + 1].wait()
        if i == 0:
            for cp in kloads[2:] + loads[1:]:
                cp.start()
        re, im = complex_product(x[...].reshape(2 * beams, x.shape[2]), kc[i], beams)
        r0[i][pl.ds(RIM_BLK, blocks0), :, pl.ds(0, Q)] = re.astype(BF16).reshape(blocks0, BLK, Q)
        r0[i][pl.ds(RIM_BLK, blocks0), :, pl.ds(Q, Q)] = im.astype(BF16).reshape(blocks0, BLK, Q)
        if i == 0:
            pl.semaphore_wait(barrier, 2 + pair_count(1))
            announce(0)
            o_cp = send(ownh, other, o_ssem, o_rsem, across)
        r_cps.append(rims(r0, i, blocks0, r_ssem, r_rsem))
        if i == 2:
            heard(0)
            announce(1)
    heard(1)
    announce(2)

    order = []
    for k in range(n_beam // 2 - 1, n_beam // 4 - 1, -1):
        order += [k, n_beam - k]
    order.append(n_beam // 2)
    for k in range(n_beam // 4 - 1, 0, -1):
        order += [k, n_beam - k]
    order.append(0)
    n_own = own.shape[0]

    def places(row):
        table = []
        for k in order:
            d = lax.rem(z + k, n_beam)
            one = two = jnp.int32(n_own)
            for o in reversed(range(n_own)):
                hit = row[o] == d
                two = jnp.where(hit, one, two)
                one = jnp.where(hit, jnp.int32(o), one)
            table.append((one, two))
        return table

    for cp in tables:
        cp.wait()
    own_places = places(own)
    o_cp.wait_recv()
    across_places = places(other)
    for buf in (px, yo):
        buf[n_own] = jnp.zeros((OS, 2 * Q), BF16)

    def window(starts, j, blocks):
        at = starts[j, ap] - (blocks * z - RIM_BLK)
        return jnp.minimum(jnp.maximum(at, 2 * j), 2 * j + 4)

    def turn(src, dst, lo, hi):
        for j in range(lo, hi):
            for c in range(2):
                dst[j, c] = src[j, c].T

    n0 = w0.shape[0]
    n1 = w1.shape[0]
    loads[1].wait()
    turn(w0t, w0, 0, n0)
    loads[2].wait()
    blocks1 = n0 * PS // BLK
    q_cps = []
    l_cps = []
    for i in range(4):
        rims_in(r_cps[i])
        clear_ends(r0, i, blocks0)
        u = i // 2
        if i % 2:
            q_cps[u].wait_recv()
        for j in range(n0):
            at = window(st0, j, blocks0)
            re, im = complex_product(w0[j].reshape(2 * PS, WIN), r0[i][pl.ds(at, NW)].reshape(WIN, 2 * Q), PS)
            rows = pl.ds(j * PS, PS)
            if i % 2 == 0:
                s0[u, rows, pl.ds(0, Q)] = re.astype(BF16)
                s0[u, rows, pl.ds(Q, Q)] = im.astype(BF16)
            else:
                to = pl.ds(RIM_BLK + j * PS // BLK, PS // BLK)
                for part, lanes in ((re, pl.ds(0, Q)), (im, pl.ds(Q, Q))):
                    both = part.astype(BF16).astype(F32) + q0[u, rows, lanes].astype(F32)
                    l1[u][to, :, lanes] = both.astype(BF16).reshape(PS // BLK, BLK, Q)
        if i % 2 == 0:
            q_cps.append(send(s0.at[u], q0.at[u], q_ssem.at[u], q_rsem.at[u], core))
        else:
            l_cps.append(rims(l1, u, blocks1, l_ssem, l_rsem))
        if i < 2:
            if i == 0:
                heard(2)
                announce(3)
            turn(w1t, w1, i * n1 // 2, (i + 1) * n1 // 2)

    x_cps = []
    for u in range(2):
        rims_in(l_cps[u])
        clear_ends(l1, u, blocks1)
        dst = yo if u else px
        for j in range(n1):
            at = window(st1, j, blocks1)
            re, im = complex_product(w1[j].reshape(2 * PS, WIN), l1[u][pl.ds(at, NW)].reshape(WIN, 2 * Q), PS)
            sectors = pl.ds(j * PS // OS, PS // OS)
            dst[sectors, :, pl.ds(0, Q)] = re.astype(BF16).reshape(PS // OS, OS, Q)
            dst[sectors, :, pl.ds(Q, Q)] = im.astype(BF16).reshape(PS // OS, OS, Q)
        if u == 0:
            for n in range(n_beam):
                for c in range(2):
                    sx[n, c] = px[across_places[n][c]]
                x_cps.append(send(sx.at[n], rx.at[n], x_ssem.at[n], x_rsem.at[n], across))

    heard(3)

    mine = pl.ds(2 * z, 2)
    a_cps = []
    for n, k in enumerate(order):
        d = lax.rem(z + k, n_beam)
        x_cps[n].wait_recv()
        for c in range(2):
            sector = (yo[own_places[n][c]].astype(F32) + rx[n, c].astype(F32)).astype(BF16)
            og[2 * d + c, 0] = sector[:, :Q]
            og[2 * d + c, 1] = sector[:, Q:]
        if k:
            a_cps.append(send(og.at[pl.ds(2 * d, 2)], out.at[mine], a_ssem.at[n], a_rsem.at[n], (ap, d)))
    local = pltpu.make_async_copy(og.at[mine], out.at[mine], o_sem)
    local.start()
    local.wait()
    for cp in a_cps:
        cp.wait()
    o_cp.wait_send()
    for cps in r_cps + l_cps:
        rims_out(cps)
    for cp in q_cps + x_cps:
        cp.wait_send()


def local(subimages, range_kernel, weights0, starts0, weights1, starts1, owners):
    beams, rng = subimages.shape[2], subimages.shape[3]
    n0, n1 = weights0.shape[1], weights1.shape[1]
    n_own = owners.shape[1]
    n_beam = lax.axis_size("beam")
    slots = 2 * n_beam
    hbm = pl.BlockSpec(memory_space=pl.ANY)
    dma = pltpu.SemaphoreType.DMA
    merged = pl.pallas_call(
        kernel,
        out_shape=pltpu.VMEM((slots, 2, OS, Q), BF16),
        in_specs=[hbm] * 7,
        out_specs=pl.BlockSpec(memory_space=pltpu.VMEM),
        scratch_shapes=[
            pltpu.VMEM((2, beams, rng), BF16),
            pltpu.VMEM((4, rng, 2 * Q), BF16),
            pltpu.VMEM((n0, 2, WIN, PS), BF16),
            pltpu.VMEM((n1, 2, WIN, PS), BF16),
            pltpu.VMEM((n0, 2, PS, WIN), BF16),
            pltpu.VMEM((n1, 2, PS, WIN), BF16),
            pltpu.VMEM((beams // BLK + 2 * RIM_BLK, BLK, 2 * Q), BF16),
            pltpu.VMEM((beams // BLK + 2 * RIM_BLK, BLK, 2 * Q), BF16),
            pltpu.VMEM((beams // BLK + 2 * RIM_BLK, BLK, 2 * Q), BF16),
            pltpu.VMEM((beams // BLK + 2 * RIM_BLK, BLK, 2 * Q), BF16),
            pltpu.VMEM((2, n0 * PS, 2 * Q), BF16),
            pltpu.VMEM((2, n0 * PS, 2 * Q), BF16),
            pltpu.VMEM((n0 * PS // BLK + 2 * RIM_BLK, BLK, 2 * Q), BF16),
            pltpu.VMEM((n0 * PS // BLK + 2 * RIM_BLK, BLK, 2 * Q), BF16),
            pltpu.VMEM((n_beam, 2, OS, 2 * Q), BF16),
            pltpu.VMEM((n_beam, 2, OS, 2 * Q), BF16),
            pltpu.VMEM((n_own + 1, OS, 2 * Q), BF16),
            pltpu.VMEM((n_own + 1, OS, 2 * Q), BF16),
            pltpu.VMEM((slots, 2, OS, Q), BF16),
            pltpu.SMEM(starts0.shape[::-1], jnp.int32),
            pltpu.SMEM(starts1.shape[::-1], jnp.int32),
            pltpu.SMEM((n_own,), jnp.int32),
            pltpu.SMEM((n_own,), jnp.int32),
            dma((6,)),
            dma((8,)),
            dma((4, 2)),
            dma((4, 2)),
            dma((2,)),
            dma((2,)),
            dma((2, 2)),
            dma((2, 2)),
            dma((n_beam,)),
            dma((n_beam,)),
            dma((n_beam - 1,)),
            dma((n_beam - 1,)),
            dma,
            dma,
            dma,
            pltpu.SemaphoreType.REGULAR((4,)),
        ],
        compiler_params=pltpu.CompilerParams(collective_id=0, has_side_effects=True),
    )(
        subimages,
        range_kernel,
        jnp.swapaxes(weights0, 3, 4),
        jnp.swapaxes(weights1, 3, 4),
        starts0.T,
        starts1.T,
        owners.reshape(n_own),
    )
    return merged[None]


def solution(mesh):
    return jax.shard_map(
        local,
        mesh=mesh,
        in_specs=(
            P("aperture", None, "beam", None),
            P("aperture", None, None, None),
            P("aperture", "beam", None, None, None),
            P(None, "beam"),
            P("aperture", "beam", None, None, None),
            P(None, "beam"),
            P("aperture", "beam", None),
        ),
        out_specs=P("aperture", "beam", None, None, None),
        check_vma=False,
    )
```
